32 devices in a mesh: dp: 4 (over z), ctx: 8 (over y, x, core).
Axes of the slice: x: 2, y: 2, z: 4, core: 2. Of those that a mesh axis runs over, the one named last changes fastest.
Arguments:
- query_stream: bfloat16 [4, 3072, 4096], P('dp', 'ctx'), may hold values from -6 to 6
- key_stream: bfloat16 [4, 3072, 4096], P('dp', 'ctx'), may hold values from -6 to 6
- value_stream: bfloat16 [4, 3072, 4096], P('dp', 'ctx'), may hold values from -6 to 6
- pole_rate: float32 [256, 16], replicated, may hold values from 6.4778646e-06 to 0.0401
- residue: float32 [256, 16], replicated, may hold values from -0.21220275 to 0.21220275
- skip_gain: float32 [4096], replicated, may hold values from 0.5 to 1.5
- out_weight: bfloat16 [4096, 4096], P(('dp', 'ctx')), may hold values from -0.09375 to 0.09375
Outputs:
- projected: bfloat16 [4, 3072, 4096], P('dp', 'ctx')
The draws below stay inside these ranges and needn't reach their ends.
All inputs are finite; a program needn't handle non-finite values.
Results may differ from the reference program's by a relative error of at most 0.007.
Values may be sent and summed in bfloat16 or wider, within the bound.
No kernel may reach another device: no remote copies, remote signals or barrier semaphores. Data moves between devices by JAX's collectives and lax.ppermute only.
A program may use at most 192 MiB of HBM per device.

```python
import math
import jax
import jax.numpy as jnp
from jax import lax

CH = 4096
DOUT = 4096
POLES = 16
BLOCK = 128
GROUPS = 256
LENGTH = 3072
SEQS = 4


def draw_poles(key):
    base = jax.random.fold_in(key, 7)
    first, second = jax.random.split(base, 2)
    lowest = math.log(0.02 / LENGTH)
    highest = math.log(0.04)
    spread = jax.random.uniform(first, (GROUPS, POLES), jnp.float32)
    levels = lowest + spread * (highest - lowest)
    base_draw = jax.random.truncated_normal(second, -3.0, 3.0, (GROUPS, POLES), jnp.float32)
    rates = jnp.exp(levels)
    effective = jnp.maximum(rates, 1.0 / LENGTH)
    residues = base_draw * jnp.sqrt(2.0 * effective / POLES)
    return (rates, residues)


def draw_pole_rate(key, part):
    return draw_poles(key)[0]


def draw_residue(key, part):
    return draw_poles(key)[1]


def block_levels(rng, extent, pieces, low, largest):
    def one(position, shards_of):
        heights = jax.random.uniform(jax.random.fold_in(jax.random.fold_in(rng, 6), position), (shards_of,), jnp.float32, low / len(pieces), largest / len(pieces))
        return jnp.repeat(jnp.exp(heights), extent[position] // shards_of).reshape((-1,) + (1,) * (len(extent) - position - 1))

    loudness = one(*pieces[0])
    for cut in pieces[1:]:
        loudness = loudness * one(*cut)
    return loudness


def noise(key, dims, deviation, reach, pieces=(), held_as=jnp.bfloat16):
    array = jax.random.normal(key, dims, jnp.float32) * deviation
    if len(pieces) > 0:
        array = block_levels(key, dims, pieces, -0.22, 0.18) * array
    return jnp.clip(array, min=-reach, max=reach).astype(held_as)


def setup_inputs(seed: int = 0) -> dict:
    seeds = jax.random.split(jax.random.key(seed), 8)
    query_stream = noise(seeds[0], (SEQS, LENGTH, CH), 1.0, 6.0, ((0, 4), (1, 8)))
    key_stream = noise(seeds[1], (SEQS, LENGTH, CH), 1.0, 6.0, ((0, 4), (1, 8)))
    value_stream = noise(seeds[2], (SEQS, LENGTH, CH), 1.0, 6.0, ((0, 4), (1, 8)))
    pole_rate = draw_pole_rate(jax.random.fold_in(seeds[7], 71), 0)
    residue = draw_residue(jax.random.fold_in(seeds[7], 71), 0)
    skip_gain = jnp.clip(jax.random.uniform(seeds[5], (CH,), jnp.float32, 0.5, 1.5), 0.5, 1.5)
    out_weight = noise(seeds[6], (CH, DOUT), CH ** -0.5, 0.09375, ((0, 32),))
    return {"query_stream": query_stream, "key_stream": key_stream, "value_stream": value_stream, "pole_rate": pole_rate, "residue": residue, "skip_gain": skip_gain, "out_weight": out_weight}


def sequence_conv(driven, pole_rate, residue, skip_gain):
    groups = pole_rate.shape[0]
    members = driven.shape[1] // groups
    span = BLOCK
    blocks = LENGTH // span
    exact_result = lax.Precision.HIGHEST
    lags = jnp.arange(span, dtype=jnp.float32)
    taps = jnp.sum(residue[:, :, None] * jnp.exp(-pole_rate[:, :, None] * lags[None, None, :]), axis=1)
    taps = taps.astype(jnp.bfloat16).astype(jnp.float32)
    diff = jnp.arange(span, dtype=jnp.int32)[:, None] - jnp.arange(span, dtype=jnp.int32)[None, :]
    shift_matrix = jnp.where(diff[None] >= 0, taps[:, jnp.clip(diff, 0, span - 1)], jnp.float32(0.0))
    ending = jnp.exp(-pole_rate[:, :, None] * (span - 1.0 - lags[None, None, :]))
    filter_extent = residue[:, :, None] * jnp.exp(-pole_rate[:, :, None] * (lags[None, None, :] + 1.0))
    block_decay = jnp.exp(-pole_rate * span)
    tiles = driven.reshape(blocks, span, groups, members)

    def advance(running_state, tile):
        near = jnp.einsum('gts,sgc->tgc', shift_matrix, tile, precision=exact_result)
        distant_part = jnp.einsum('odf,odz->foz', filter_extent, running_state, precision=exact_result)
        fresh = jnp.einsum('grs,sgc->grc', ending, tile, precision=exact_result)
        running_state = block_decay[:, :, None] * running_state + fresh
        return running_state, near + distant_part

    start = jnp.zeros((groups, pole_rate.shape[1], members), jnp.float32)
    _, output = lax.scan(advance, start, tiles)
    return output.reshape(LENGTH, groups * members) + skip_gain[None, :] * driven


def reference(query_stream, key_stream, value_stream, pole_rate, residue, skip_gain, out_weight):
    weight_full = out_weight.astype(jnp.float32)

    def one_sequence(items):
        query_rows, key_rows, value_rows = items
        driven = (key_rows.astype(jnp.float32) * value_rows.astype(jnp.float32)).astype(jnp.bfloat16).astype(jnp.float32)
        conv = sequence_conv(driven, pole_rate, residue, skip_gain)
        gated = (query_rows.astype(jnp.float32) * conv).astype(jnp.bfloat16)
        summed = jnp.dot(gated.astype(jnp.float32), weight_full, precision=lax.Precision.HIGHEST, preferred_element_type=jnp.float32)
        return summed.astype(jnp.bfloat16)

    return lax.map(one_sequence, (query_stream, key_stream, value_stream))
```

```python
import jax
import jax.numpy as jnp
import numpy as np
from jax import lax
from jax.experimental import pallas as pl
from jax.experimental.pallas import tpu as pltpu
from jax.sharding import PartitionSpec as P

BLOCK = 128
LANES = 128
COLS = 256
F32 = jnp.float32
BF16 = jnp.bfloat16
AXES = ("dp", "ctx")
fence = lax.optimization_barrier


def params(mib):
    return pltpu.CompilerParams(vmem_limit_bytes=mib << 20, dimension_semantics=("arbitrary",))


def split(a):
    high = a.astype(BF16)
    return high, (a - high.astype(F32)).astype(BF16)


def iota(shape, axis):
    return lax.broadcasted_iota(jnp.int32, shape, axis)


def state_kernel(members, poles, blocks, k_ref, v_ref, col_ref, lane_ref, d_ref, bs_ref, slab_ref):
    per = LANES // members
    for sub in range(k_ref.shape[1] // LANES):
        at = slice(sub * LANES, (sub + 1) * LANES)
        d = (k_ref[:, at].astype(F32) * v_ref[:, at].astype(F32)).astype(BF16)
        d_ref[:, at] = d
        rate = col_ref[sub * per * poles : (sub + 1) * per * poles, 0:1]
        back = (BLOCK - 1 - iota((per * poles, BLOCK), 1)).astype(F32)
        ending = jnp.concatenate(split(jnp.exp(-rate * back)), axis=0)
        tiles = jnp.concatenate([d[b * BLOCK : (b + 1) * BLOCK] for b in range(blocks)], axis=1)
        part = jnp.dot(ending, tiles, preferred_element_type=F32)
        part = part[: per * poles] + part[per * poles :]
        same = iota(part.shape, 0) // poles == (iota(part.shape, 1) % LANES) // members
        state = jnp.where(same, part, 0.0).reshape(per, poles, blocks * LANES).sum(axis=0)
        decay = jnp.exp(-lane_ref[:, at] * BLOCK)
        slab = None
        for b in range(blocks):
            one = state[:, b * LANES : (b + 1) * LANES]
            bs_ref[b * poles : (b + 1) * poles, at] = one
            slab = one if slab is None else slab * decay + one
        slab_ref[:, at] = slab


def conv_kernel(
    members, poles, blocks, d_ref, q_ref, col_ref, row_ref, bs_ref, inc_ref, lane_ref, skip_ref, g_ref
):
    per = LANES // members
    wide = per * poles
    for sub in range(d_ref.shape[1] // LANES):
        at = slice(sub * LANES, (sub + 1) * LANES)
        rate = col_ref[sub * wide : (sub + 1) * wide, 0:1]
        residue = col_ref[sub * wide : (sub + 1) * wide, 1:2]
        lag = ((BLOCK - iota((wide, BLOCK), 1)) % BLOCK).astype(F32)
        base = (residue * jnp.exp(-rate * lag)).reshape(per, poles, BLOCK).sum(axis=1)
        base = base.astype(BF16).astype(F32)
        causal = iota((BLOCK, BLOCK), 1) <= iota((BLOCK, BLOCK), 0)
        left = []
        for g in range(per):
            rows = jnp.broadcast_to(base[g : g + 1], (BLOCK, BLOCK))
            rows = pltpu.roll(rows, 0, 1, stride=1, stride_axis=0)
            left.append(jnp.where(causal, rows, 0.0).astype(BF16))
        ahead = (iota((BLOCK, wide), 0) + 1).astype(F32)
        at_row = slice(sub * wide, (sub + 1) * wide)
        reach = row_ref[1:2, at_row] * jnp.exp(-row_ref[0:1, at_row] * ahead)
        high, low = split(reach)
        left = jnp.concatenate(left + [high, low, high], axis=1)
        decay = jnp.exp(-lane_ref[:, at] * BLOCK)
        same = iota((wide, LANES), 0) // poles == iota((wide, LANES), 1) // members
        owner = iota((1, LANES), 1) // members
        state = inc_ref[:, at]
        right = []
        for b in range(blocks):
            tile = d_ref[b * BLOCK : (b + 1) * BLOCK, at]
            spread = jnp.where(same, jnp.concatenate([state] * per, axis=0), 0.0)
            s_high, s_low = split(spread)
            masked = [tile * jnp.where(owner == g, 1.0, 0.0).astype(BF16) for g in range(per)]
            right.append(jnp.concatenate(masked + [s_high, s_high, s_low], axis=0))
            if b + 1 < blocks:
                state = state * decay + bs_ref[b * poles : (b + 1) * poles, at]
        conv = jnp.dot(left, jnp.concatenate(right, axis=1), preferred_element_type=F32)
        for b in range(blocks):
            rows = slice(b * BLOCK, (b + 1) * BLOCK)
            whole = conv[:, b * LANES : (b + 1) * LANES] + skip_ref[:, at] * d_ref[rows, at].astype(F32)
            g_ref[sub, rows, :] = (q_ref[rows, at].astype(F32) * whole).astype(BF16)


def states(key, value, col, lane, members, poles):
    rows, width = key.shape
    blocks = rows // BLOCK
    step = 2 * LANES
    seq = pl.BlockSpec((rows, step), lambda i: (0, i))
    wide = step // members * poles
    return pl.pallas_call(
        lambda *refs: state_kernel(members, poles, blocks, *refs),
        grid=(width // step,),
        in_specs=[
            seq,
            seq,
            pl.BlockSpec((wide, 2), lambda i: (i, 0)),
            pl.BlockSpec((poles, step), lambda i: (0, i)),
        ],
        out_specs=[
            seq,
            pl.BlockSpec((blocks * poles, step), lambda i: (0, i)),
            pl.BlockSpec((poles, step), lambda i: (0, i)),
        ],
        out_shape=[
            jax.ShapeDtypeStruct((rows, width), BF16),
            jax.ShapeDtypeStruct((blocks * poles, width), F32),
            jax.ShapeDtypeStruct((poles, width), F32),
        ],
        compiler_params=params(32),
        name="states",
    )(key, value, col, lane)


def convolve(driven, query, col, row, block_state, incoming, lane, skip, members, poles):
    rows, width = driven.shape
    blocks = rows // BLOCK
    step = 2 * LANES
    seq = pl.BlockSpec((rows, step), lambda i: (0, i))
    wide = step // members * poles
    return pl.pallas_call(
        lambda *refs: conv_kernel(members, poles, blocks, *refs),
        grid=(width // step,),
        in_specs=[
            seq,
            seq,
            pl.BlockSpec((wide, 2), lambda i: (i, 0)),
            pl.BlockSpec((2, wide), lambda i: (0, i)),
            pl.BlockSpec((blocks * poles, step), lambda i: (0, i)),
            pl.BlockSpec((poles, step), lambda i: (0, i)),
            pl.BlockSpec((poles, step), lambda i: (0, i)),
            pl.BlockSpec((1, step), lambda i: (0, i)),
        ],
        out_specs=pl.BlockSpec((step // LANES, rows, LANES), lambda i: (i, 0, 0)),
        out_shape=jax.ShapeDtypeStruct((width // LANES, rows, LANES), BF16),
        compiler_params=params(32),
        name="convolve",
    )(driven, query, col, row, block_state, incoming, lane, skip)


def incoming_state(total, lane, rows, slabs):
    place = lax.axis_index("ctx")
    before = jnp.zeros_like(total)
    width = 1
    while width < slabs:
        other = lax.ppermute(total, "ctx", [(i, i ^ width) for i in range(slabs)])
        upper = (place // width) % 2 == 1
        offset = (place % width).astype(F32) * rows
        before = jnp.where(upper, before + other * jnp.exp(-lane * offset), before)
        decay = jnp.exp(-lane * float(rows * width))
        total = jnp.where(upper, other * decay + total, total * decay + other)
        width *= 2
    return before


def project_kernel(count, started, idx_ref, own_ref, peer_ref, *refs):
    pieces, refs = refs[:count], refs[count:]
    sums = None
    if started:
        sums = [refs[0][...], refs[1][...]]
        refs = refs[2:]
    for p in range(0, count, 2):
        weight = jnp.concatenate([pieces[p][0], pieces[p + 1][0]], axis=0)
        first, second = idx_ref[p], idx_ref[p + 1]
        parts = []
        for g_ref in (own_ref, peer_ref):
            gated = jnp.concatenate([g_ref[first], g_ref[second]], axis=1)
            parts.append(jnp.dot(gated, weight, preferred_element_type=F32))
        sums = parts if sums is None else [a + b for a, b in zip(sums, parts)]
    for o_ref, s in zip(refs, sums):
        o_ref[...] = s.astype(o_ref.dtype)


def project(idx, own, peer, pieces, wide, sums=None, dtype=F32):
    shards, rows, depth = own.shape
    count = len(pieces)
    whole = pl.BlockSpec((shards, rows, depth), lambda b, i: (0, 0, 0), pipeline_mode=pl.Buffered(1))
    block = pl.BlockSpec((rows, COLS), lambda b, i: (0, b))
    specs = [pl.BlockSpec((1, depth, COLS), lambda b, i, s=s: (s + b, 0, 0)) for _, s in pieces]
    started = sums is not None
    return pl.pallas_call(
        lambda *refs: project_kernel(count, started, *refs),
        grid_spec=pltpu.PrefetchScalarGridSpec(
            num_scalar_prefetch=1,
            grid=(wide // COLS,),
            in_specs=[whole, whole] + specs + [block] * (2 * started),
            out_specs=[block, block],
        ),
        out_shape=[jax.ShapeDtypeStruct((rows, wide), dtype)] * 2,
        compiler_params=params(48),
        name="project",
    )(idx, own, peer, *[a for a, _ in pieces], *(sums or ()))


def swap(a, devices, bit):
    return lax.ppermute(a, AXES, [(i, i ^ bit) for i in range(devices)])


def ahead(a, devices):
    return lax.ppermute(a, AXES, [(i, (i + 8) % devices) for i in range(devices)])


def local(mesh_shape, query_stream, key_stream, value_stream, pole_rate, residue, skip_gain, out_weight):
    seqs, rows, width = query_stream.shape
    groups, poles = pole_rate.shape
    members = width // groups
    slabs = mesh_shape["ctx"]
    devices = mesh_shape["dp"] * slabs
    depth, dout = out_weight.shape
    query, key, value = [a.reshape(rows, width) for a in (query_stream, key_stream, value_stream)]
    col = jnp.stack([pole_rate.reshape(-1), residue.reshape(-1)], axis=1)
    row = jnp.stack([pole_rate.reshape(-1), residue.reshape(-1)], axis=0)
    lane = jnp.repeat(pole_rate.T, members, axis=1)
    skip = skip_gain[None]

    if depth != LANES:
        driven, block_state, slab = states(key, value, col, lane, members, poles)
        incoming = incoming_state(slab, lane, rows, slabs)
        gated = convolve(driven, query, col, row, block_state, incoming, lane, skip, members, poles)
        weight = lax.all_gather(out_weight, AXES, axis=0, tiled=True)
        flat = gated.transpose(1, 0, 2).reshape(rows, width)
        out = jnp.dot(flat, weight, preferred_element_type=F32)
        return out.astype(BF16).reshape(seqs, rows, dout)

    place = lax.axis_index(AXES)
    core = place % 2
    half = dout // 2
    nb = half // COLS
    ring = devices // 8
    tiles = out_weight.reshape(depth, 2 * nb, COLS).transpose(1, 0, 2)
    mine = lax.dynamic_slice_in_dim(tiles, core * nb, nb, 0)
    give = lax.dynamic_slice_in_dim(tiles, (1 - core) * nb, nb, 0)
    got = swap(give, devices, 1)

    pieces = [(mine, 0, (0, 0, 0, 0)), (got, 0, (0, 0, 0, 1))]
    late = []
    cur = (mine, got)
    prev = None
    work = (key, value)
    for r in range(ring + 1):
        pay_x, pay_y = [], []
        if prev is not None:
            (a, ax), (b, by) = prev
            pay_x += [b, by]
            pay_y += [a, ax]
        if r < ring:
            pay_x.append(cur[0])
            pay_y.append(cur[1])
        pay_x = jnp.concatenate(pay_x, axis=0)
        pay_y = jnp.concatenate(pay_y, axis=0)
        pay_z = jnp.concatenate(cur, axis=0) if r + 1 < ring else None
        pay_x, pay_y, pay_z, work = fence((pay_x, pay_y, pay_z, work))
        new_z = ahead(pay_z, devices) if pay_z is not None else None
        new_x = swap(pay_x, devices, 2)
        new_y = swap(pay_y, devices, 4)
        if r == 0:
            work = states(*work, col, lane, members, poles)
        elif r == 1:
            driven, block_state, slab = work
            work = (driven, block_state, incoming_state(slab, lane, rows, slabs))
        elif r == 2:
            driven, block_state, incoming = work
            work = convolve(driven, query, col, row, block_state, incoming, lane, skip, members, poles)
        elif r == ring - 1:
            own = work
            work = (own, swap(own, devices, 1))
        elif r == ring:
            table = [p for p in pieces]
            idx = shard_table(place, ring, [p[2] for p in table])
            work = (work, project(idx, *work, [p[:2] for p in table], half))
        new_x, new_y, new_z, work = fence((new_x, new_y, new_z, work))
        at = 0
        if prev is not None:
            late = [
                (new_x, 0, (r - 1, 0, 1, 1)),
                (new_x, nb, (r - 1, 1, 1, 1)),
                (new_y, 0, (r - 1, 1, 0, 0)),
                (new_y, nb, (r - 1, 1, 1, 0)),
            ]
            if r < ring:
                pieces += late
            at = 2 * nb
        if r < ring:
            pieces += [(new_x, at, (r, 0, 1, 0)), (new_y, at, (r, 1, 0, 1))]
            prev = ((cur[0], new_x[at:]), (cur[1], new_y[at:]))
        if new_z is not None:
            pieces += [(new_z, 0, (r + 1, 0, 0, 0)), (new_z, nb, (r + 1, 0, 0, 1))]
            cur = (new_z[:nb], new_z[nb:])
    (own, peer), sums = work
    idx = shard_table(place, ring, [p[2] for p in late])
    out_own, out_peer = project(idx, own, peer, [p[:2] for p in late], half, sums, BF16)
    other = swap(out_peer, devices, 1)
    out = jnp.where(
        core == 0,
        jnp.concatenate([out_own, other], axis=1),
        jnp.concatenate([other, out_own], axis=1),
    )
    return out.reshape(seqs, rows, dout)


def shard_table(place, ring, steps):
    steps = np.asarray(steps, np.int32)
    z = (place // 8 + ring - steps[:, 0]) % ring
    low = (place % 8) ^ jnp.asarray(steps[:, 1] * 4 + steps[:, 2] * 2 + steps[:, 3])
    return (z * 8 + low).astype(jnp.int32)


def solution(mesh):
    shape = dict(mesh.shape)
    return jax.shard_map(
        lambda *args: local(shape, *args),
        mesh=mesh,
        in_specs=(
            P("dp", "ctx", None),
            P("dp", "ctx", None),
            P("dp", "ctx", None),
            P(),
            P(),
            P(),
            P(("dp", "ctx"), None),
        ),
        out_specs=P("dp", "ctx", None),
        check_vma=False,
    )
```

```python
import jax
import jax.numpy as jnp
import numpy as np
from jax import lax
from jax.experimental import pallas as pl
from jax.experimental.pallas import tpu as pltpu
from jax.sharding import PartitionSpec as P

BLOCK = 128
LANES = 128
COLS = 512
SCALE = 4
F32 = jnp.float32
BF16 = jnp.bfloat16
AXES = ("dp", "ctx")
fence = lax.optimization_barrier


def params(mib):
    return pltpu.CompilerParams(vmem_limit_bytes=mib << 20, dimension_semantics=("arbitrary",))


def cost(flops, moved):
    return pl.CostEstimate(flops=int(flops), transcendentals=0, bytes_accessed=int(moved))


def split(a):
    high = a.astype(BF16)
    return high, (a - high.astype(F32)).astype(BF16)


def in_hbm(a):
    return pltpu.with_memory_space_constraint(a, pltpu.HBM)


def iota(shape, axis):
    return lax.broadcasted_iota(jnp.int32, shape, axis)


def state_kernel(members, poles, blocks, k_ref, v_ref, col_ref, lane_ref, d_ref, bs_ref, slab_ref):
    per = LANES // members
    for sub in range(k_ref.shape[1] // LANES):
        at = slice(sub * LANES, (sub + 1) * LANES)
        d = (k_ref[:, at].astype(F32) * v_ref[:, at].astype(F32)).astype(BF16)
        d_ref[:, at] = d
        rate = col_ref[sub * per * poles : (sub + 1) * per * poles, 0:1]
        back = (BLOCK - 1 - iota((per * poles, BLOCK), 1)).astype(F32)
        ending = jnp.concatenate(split(jnp.exp(-rate * back)), axis=0)
        tiles = jnp.concatenate([d[b * BLOCK : (b + 1) * BLOCK] for b in range(blocks)], axis=1)
        part = jnp.dot(ending, tiles, preferred_element_type=F32)
        part = part[: per * poles] + part[per * poles :]
        same = iota(part.shape, 0) // poles == (iota(part.shape, 1) % LANES) // members
        state = jnp.where(same, part, 0.0).reshape(per, poles, blocks * LANES).sum(axis=0)
        decay = jnp.exp(-lane_ref[:, at] * BLOCK)
        slab = None
        for b in range(blocks):
            one = state[:, b * LANES : (b + 1) * LANES]
            bs_ref[b * poles : (b + 1) * poles, at] = one
            slab = one if slab is None else slab * decay + one
        slab_ref[:, at] = slab


def conv_kernel(
    members, poles, blocks, d_ref, q_ref, col_ref, row_ref, bs_ref, inc_ref, lane_ref, skip_ref, g_ref
):
    per = LANES // members
    wide = per * poles
    for sub in range(d_ref.shape[1] // LANES):
        at = slice(sub * LANES, (sub + 1) * LANES)
        rate = col_ref[sub * wide : (sub + 1) * wide, 0:1]
        residue = col_ref[sub * wide : (sub + 1) * wide, 1:2]
        lag = ((BLOCK - iota((wide, BLOCK), 1)) % BLOCK).astype(F32)
        base = (residue * jnp.exp(-rate * lag)).reshape(per, poles, BLOCK).sum(axis=1)
        base = base.astype(BF16).astype(F32)
        causal = iota((BLOCK, BLOCK), 1) <= iota((BLOCK, BLOCK), 0)
        left = []
        for g in range(per):
            rows = jnp.broadcast_to(base[g : g + 1], (BLOCK, BLOCK))
            rows = pltpu.roll(rows, 0, 1, stride=1, stride_axis=0)
            left.append(jnp.where(causal, rows, 0.0).astype(BF16))
        ahead = (iota((BLOCK, wide), 0) + 1).astype(F32)
        at_row = slice(sub * wide, (sub + 1) * wide)
        reach = row_ref[1:2, at_row] * jnp.exp(-row_ref[0:1, at_row] * ahead)
        high, low = split(reach)
        left = jnp.concatenate(left + [high, low, high], axis=1)
        decay = jnp.exp(-lane_ref[:, at] * BLOCK)
        same = iota((wide, LANES), 0) // poles == iota((wide, LANES), 1) // members
        owner = iota((1, LANES), 1) // members
        state = inc_ref[:, at]
        right = []
        for b in range(blocks):
            tile = d_ref[b * BLOCK : (b + 1) * BLOCK, at]
            spread = jnp.where(same, jnp.concatenate([state] * per, axis=0), 0.0)
            s_high, s_low = split(spread)
            masked = [tile * jnp.where(owner == g, 1.0, 0.0).astype(BF16) for g in range(per)]
            right.append(jnp.concatenate(masked + [s_high, s_high, s_low], axis=0))
            if b + 1 < blocks:
                state = state * decay + bs_ref[b * poles : (b + 1) * poles, at]
        conv = jnp.dot(left, jnp.concatenate(right, axis=1), preferred_element_type=F32)
        for b in range(blocks):
            rows = slice(b * BLOCK, (b + 1) * BLOCK)
            whole = conv[:, b * LANES : (b + 1) * LANES] + skip_ref[:, at] * d_ref[rows, at].astype(F32)
            g_ref[sub, rows, :] = (q_ref[rows, at].astype(F32) * whole).astype(BF16)


def states(key, value, col, lane, members, poles):
    rows, width = key.shape
    blocks = rows // BLOCK
    step = 2 * LANES
    seq = pl.BlockSpec((rows, step), lambda i: (0, i))
    wide = step // members * poles
    return pl.pallas_call(
        lambda *refs: state_kernel(members, poles, blocks, *refs),
        grid=(width // step,),
        in_specs=[
            seq,
            seq,
            pl.BlockSpec((wide, 2), lambda i: (i, 0)),
            pl.BlockSpec((poles, step), lambda i: (0, i)),
        ],
        out_specs=[
            seq,
            pl.BlockSpec((blocks * poles, step), lambda i: (0, i)),
            pl.BlockSpec((poles, step), lambda i: (0, i)),
        ],
        out_shape=[
            jax.ShapeDtypeStruct((rows, width), BF16),
            jax.ShapeDtypeStruct((blocks * poles, width), F32),
            jax.ShapeDtypeStruct((poles, width), F32),
        ],
        compiler_params=params(32),
        cost_estimate=cost(4 * poles * members * rows * width * SCALE, 6 * rows * width),
        name="states",
    )(in_hbm(key), in_hbm(value), col, lane)


def convolve(driven, query, col, row, block_state, incoming, lane, skip, members, poles):
    rows, width = driven.shape
    blocks = rows // BLOCK
    step = 2 * LANES
    seq = pl.BlockSpec((rows, step), lambda i: (0, i))
    wide = step // members * poles
    return pl.pallas_call(
        lambda *refs: conv_kernel(members, poles, blocks, *refs),
        grid=(width // step,),
        in_specs=[
            seq,
            seq,
            pl.BlockSpec((wide, 2), lambda i: (i, 0)),
            pl.BlockSpec((2, wide), lambda i: (0, i)),
            pl.BlockSpec((blocks * poles, step), lambda i: (0, i)),
            pl.BlockSpec((poles, step), lambda i: (0, i)),
            pl.BlockSpec((poles, step), lambda i: (0, i)),
            pl.BlockSpec((1, step), lambda i: (0, i)),
        ],
        out_specs=pl.BlockSpec((step // LANES, rows, LANES), lambda i: (i, 0, 0)),
        out_shape=jax.ShapeDtypeStruct((width // LANES, rows, LANES), BF16),
        compiler_params=params(32),
        cost_estimate=cost(2 * (BLOCK * LANES // members + 3 * LANES) * rows * width * SCALE, 6 * rows * width),
        name="convolve",
    )(in_hbm(driven), in_hbm(query), col, row, block_state, incoming, lane, skip)


def scan_send(total, slabs, width):
    return lax.ppermute(total, "ctx", [(i, i ^ width) for i in range(slabs)])


def pair_total(slab, other, lane, rows, core):
    decay = jnp.exp(-lane * float(rows))
    total = jnp.where(core == 0, slab * decay + other, other * decay + slab)
    half = slab.shape[1] // 2
    return [lax.dynamic_slice_in_dim(a, core * half, half, 1) for a in (total, lane)]


def scan_step(before, total, other, lane, rows, width):
    place = lax.axis_index("ctx")
    upper = (place // width) % 2 == 1
    offset = ((place % width) // 2 * 2).astype(F32) * rows
    before = jnp.where(upper, before + other * jnp.exp(-lane * offset), before)
    decay = jnp.exp(-lane * float(rows * width))
    return before, jnp.where(upper, other * decay + total, total * decay + other)


def incoming_state(before, other_half, other_slab, lane, rows, core):
    ahead = jnp.where(
        core == 0,
        jnp.concatenate([before, other_half], axis=1),
        jnp.concatenate([other_half, before], axis=1),
    )
    return jnp.where(core == 0, ahead, ahead * jnp.exp(-lane * float(rows)) + other_slab)


def project_kernel(sizes, sides, started, idx_ref, *refs):
    shards = sum(sizes) // LANES
    gated = [refs[i * shards : (i + 1) * shards] for i in range(sides)]
    refs = refs[sides * shards :]
    weights, refs = refs[: len(sizes)], refs[len(sizes) :]
    totals = [r[...] for r in refs[:sides]] if started else [None] * sides
    outs = refs[-sides:]
    weights, at = list(weights), 0
    while weights:
        depth, rhs = 0, []
        while weights and depth + weights[0].shape[0] <= 2 * LANES:
            rhs.append(weights.pop(0)[...])
            depth += rhs[-1].shape[0]
        rhs = jnp.concatenate(rhs, axis=0) if len(rhs) > 1 else rhs[0]
        for i in range(sides):
            lhs = [r[0] for r in gated[i][at : at + depth // LANES]]
            lhs = jnp.concatenate(lhs, axis=1) if len(lhs) > 1 else lhs[0]
            part = jnp.dot(lhs, rhs, preferred_element_type=F32)
            totals[i] = part if totals[i] is None else totals[i] + part
        at += depth // LANES
    for o_ref, total in zip(outs, totals):
        o_ref[...] = total.astype(o_ref.dtype)


def project(place, ring, gated, pieces, wide, total=None, side=None, dout=None, dtype=F32):
    shards, rows, depth = gated[0].shape
    steps = [one for _, _, owners in pieces for one in owners]
    sizes = [LANES * len(owners) for _, _, owners in pieces]
    sides = len(gated)
    nb = wide // COLS
    idx = shard_table(place, ring, steps)
    if side is not None:
        idx = jnp.concatenate([idx, (side * nb).astype(jnp.int32)[None]])
    block = pl.BlockSpec((rows, COLS), lambda b, i: (0, b))
    specs = [pl.BlockSpec((1, rows, depth), lambda b, i, p=p: (i[p], 0, 0)) for p in range(len(steps))] * sides
    specs += [
        pl.BlockSpec((size, COLS), lambda b, i, at=at: (at, b)) for size, (_, at, _) in zip(sizes, pieces)
    ]
    operands = [g for g in gated for _ in steps] + [a for a, _, _ in pieces]
    if total is not None:
        specs += [block] * sides
        operands += list(total)
    operands = [in_hbm(a) for a in operands]
    last = len(steps)
    shape = jax.ShapeDtypeStruct((rows, wide if side is None else dout), dtype)
    return pl.pallas_call(
        lambda *refs: project_kernel(sizes, sides, total is not None, *refs),
        grid_spec=pltpu.PrefetchScalarGridSpec(
            num_scalar_prefetch=1,
            grid=(nb,),
            in_specs=specs,
            out_specs=[block if side is None else pl.BlockSpec((rows, COLS), lambda b, i: (0, i[last] + b))] * sides,
        ),
        out_shape=[shape] * sides,
        compiler_params=params(48),
        cost_estimate=cost(2 * len(steps) * LANES * sides * rows * wide * SCALE, 4 * sides * rows * wide),
        name="project",
    )(idx, *operands)


def local(mesh_shape, query_stream, key_stream, value_stream, pole_rate, residue, skip_gain, out_weight):
    seqs, rows, width = query_stream.shape
    groups, poles = pole_rate.shape
    members = width // groups
    slabs = mesh_shape["ctx"]
    devices = mesh_shape["dp"] * slabs
    depth, dout = out_weight.shape
    query, key, value = [a.reshape(rows, width) for a in (query_stream, key_stream, value_stream)]
    skip = skip_gain[None]

    if depth != LANES:
        core = lax.axis_index("ctx") % 2
        col, row, lane = tables(pole_rate, residue, members)
        driven, block_state, slab = states(key, value, col, lane, members, poles)
        other_slab = scan_send(slab, slabs, 1)
        total, lane_half = pair_total(slab, other_slab, lane, rows, core)
        before = jnp.zeros_like(total)
        step = 2
        while step < slabs:
            other = scan_send(total, slabs, step)
            before, total = scan_step(before, total, other, lane_half, rows, step)
            step *= 2
        incoming = incoming_state(before, scan_send(before, slabs, 1), other_slab, lane, rows, core)
        gated = convolve(driven, query, col, row, block_state, incoming, lane, skip, members, poles)
        weight = lax.all_gather(out_weight, AXES, axis=0, tiled=True)
        flat = gated.transpose(1, 0, 2).reshape(rows, width)
        out = jnp.dot(flat, weight, preferred_element_type=F32)
        return out.astype(BF16).reshape(seqs, rows, dout)

    def swap(a, bit):
        return lax.ppermute(a, AXES, [(i, i ^ bit) for i in range(devices)])

    def ahead(a):
        return lax.ppermute(a, AXES, [(i, (i + 8) % devices) for i in range(devices)])

    place = lax.axis_index(AXES)
    core = place % 2
    half = dout // 2
    ring = devices // 8
    mine = lax.dynamic_slice_in_dim(out_weight, core * half, half, 1)
    give = lax.dynamic_slice_in_dim(out_weight, (1 - core) * half, half, 1)

    got = swap(give, 1)
    cur = jnp.concatenate([mine, got], axis=0)
    both = [(0, 0, 0, 0), (0, 0, 0, 1)]
    pieces = [(cur, 0, both)]

    def straight(cur, back, last):
        new = [swap(cur, 2), swap(cur, 4)] + ([] if last else [ahead(cur)])
        owners = [[(back + dz, dy, dx, k) for k in (0, 1)] for dz, dy, dx in ((0, 0, 1), (0, 1, 0), (1, 0, 0))]
        return [(a, 0, o) for a, o in zip(new, owners)]

    def diagonal(over_x, over_y, back):
        return [(swap(over_y, 4), 0, [(back, 1, 1, 0)]), (swap(over_x, 2), 0, [(back, 1, 1, 1)])]

    def over(new):
        return new[1][0][depth:], new[0][0][:depth]

    def settle(new, work):
        arrays, work = fence(([a for a, _, _ in new], work))
        return [(a, at, o) for a, (_, at, o) in zip(arrays, new)], work

    cur, pole_rate, residue, key, value = fence((cur, pole_rate, residue, key, value))
    col, row, lane = tables(pole_rate, residue, members)
    new = straight(cur, 0, False)
    driven, block_state, slab = states(key, value, col, lane, members, poles)
    new, (driven, block_state, slab, lane) = settle(new, (driven, block_state, slab, lane))
    pieces += new
    cur = new[2][0]
    new = diagonal(*over(new), 0)
    other_slab = scan_send(slab, slabs, 1)
    total, lane_half = pair_total(slab, other_slab, lane, rows, core)
    other = scan_send(total, slabs, 2)
    before, total = scan_step(jnp.zeros_like(total), total, other, lane_half, rows, 2)
    new, (before, total, other_slab, lane_half, cur) = settle(new, (before, total, other_slab, lane_half, cur))
    pieces += new
    other = scan_send(total, slabs, 4)
    before, _ = scan_step(before, total, other, lane_half, rows, 4)
    new = straight(cur, 1, False)
    other_half = scan_send(before, slabs, 1)
    new, (before, other_half) = settle(new, (before, other_half))
    pieces += new
    back = 2
    gated = None
    while back < ring - 1:
        done = diagonal(*over(new), back - 1)
        new = done + straight(new[2][0], back, False)
        if gated is None:
            incoming = incoming_state(before, other_half, other_slab, lane, rows, core)
            gated = convolve(driven, query, col, row, block_state, incoming, lane, skip, members, poles)
        new, gated = settle(new, gated)
        pieces += new
        new = new[2:]
        back += 1
    cur = new[2][0]
    new = diagonal(*over(new), back - 1)
    peer = swap(gated, 1)
    new, (gated, peer, cur) = settle(new, (gated, peer, cur))
    pieces += new
    new = straight(cur, back, True)
    sums = project(place, ring, (gated, peer), pieces, half)
    new, (gated, peer, sums) = settle(new, (gated, peer, sums))
    late = diagonal(*over(new), back)
    sums = project(place, ring, (gated, peer), new, half, sums)
    late, (gated, peer, (sum_own, sum_peer)) = settle(late, (gated, peer, sums))
    (out_peer,) = project(place, ring, [peer], late, half, [sum_peer], dtype=BF16)
    other = swap(out_peer, 1)
    (out,) = project(place, ring, [gated], late, half, [sum_own], core, dout, dtype=BF16)
    return put(other, 1 - core, out).reshape(seqs, rows, dout)


def put_kernel(side_ref, half_ref, whole_ref, o_ref):
    o_ref[...] = half_ref[...]


def put(half, side, whole):
    rows, wide = half.shape
    nb = wide // COLS
    return pl.pallas_call(
        put_kernel,
        grid_spec=pltpu.PrefetchScalarGridSpec(
            num_scalar_prefetch=1,
            grid=(nb,),
            in_specs=[pl.BlockSpec((rows, COLS), lambda b, i: (0, b)), pl.BlockSpec(memory_space=pl.ANY)],
            out_specs=pl.BlockSpec((rows, COLS), lambda b, i: (0, i[0] * nb + b)),
        ),
        out_shape=jax.ShapeDtypeStruct(whole.shape, whole.dtype),
        input_output_aliases={2: 0},
        compiler_params=params(32),
        name="put",
    )(side.astype(jnp.int32)[None], half, whole)


def tables(pole_rate, residue, members):
    col = jnp.stack([pole_rate.reshape(-1), residue.reshape(-1)], axis=1)
    row = jnp.stack([pole_rate.reshape(-1), residue.reshape(-1)], axis=0)
    return col, row, jnp.repeat(pole_rate.T, members, axis=1)


def shard_table(place, ring, steps):
    steps = np.asarray(steps, np.int32)
    z = (place // 8 + ring - steps[:, 0]) % ring
    low = (place % 8) ^ jnp.asarray(steps[:, 1] * 4 + steps[:, 2] * 2 + steps[:, 3])
    return (z * 8 + low).astype(jnp.int32)


def solution(mesh):
    shape = dict(mesh.shape)
    return jax.shard_map(
        lambda *args: local(shape, *args),
        mesh=mesh,
        in_specs=(
            P("dp", "ctx", None),
            P("dp", "ctx", None),
            P("dp", "ctx", None),
            P(),
            P(),
            P(),
            P(("dp", "ctx"), None),
        ),
        out_specs=P("dp", "ctx", None),
        check_vma=False,
    )
```

```python
import jax
import jax.numpy as jnp
import numpy as np
from jax import lax
from jax.experimental import pallas as pl
from jax.experimental.pallas import tpu as pltpu
from jax.sharding import PartitionSpec as P

BLOCK = 128
LANES = 128
COLS = 512
SCALE = 4
STEP = 1024
F32 = jnp.float32
BF16 = jnp.bfloat16
AXES = ("dp", "ctx")
fence = lax.optimization_barrier


def params(mib):
    return pltpu.CompilerParams(vmem_limit_bytes=mib << 20, dimension_semantics=("arbitrary",))


def cost(flops, moved):
    return pl.CostEstimate(flops=int(flops), transcendentals=0, bytes_accessed=int(moved))


def split(a):
    high = a.astype(BF16)
    return high, (a - high.astype(F32)).astype(BF16)


def in_hbm(a):
    return pltpu.with_memory_space_constraint(a, pltpu.HBM)


def iota(shape, axis):
    return lax.broadcasted_iota(jnp.int32, shape, axis)


def lane_rate(rate, same, per, poles):
    return jnp.where(same, rate, 0.0).reshape(per, poles, same.shape[1]).sum(axis=0)


def state_kernel(members, poles, blocks, k_ref, v_ref, col_ref, d_ref, bs_ref, slab_ref):
    per = LANES // members
    wide = per * poles
    back = (BLOCK - 1 - iota((wide, BLOCK), 1)).astype(F32)
    same = iota((wide, LANES), 0) // poles == iota((wide, LANES), 1) // members
    for sub in range(k_ref.shape[1] // LANES):
        at = slice(sub * LANES, (sub + 1) * LANES)
        d = (k_ref[:, at].astype(F32) * v_ref[:, at].astype(F32)).astype(BF16)
        d_ref[:, at] = d
        rate = col_ref[sub * wide : (sub + 1) * wide, 0:1]
        ending = jnp.concatenate(split(jnp.exp(-rate * back)), axis=1)
        tiles = jnp.concatenate([d[b * BLOCK : (b + 1) * BLOCK] for b in range(blocks)], axis=1)
        tiles = jnp.concatenate([tiles, tiles], axis=0)
        part = jnp.dot(ending, tiles, preferred_element_type=F32)
        decay = jnp.exp(-lane_rate(rate, same, per, poles) * BLOCK)
        slab = None
        for b in range(blocks):
            one = jnp.where(same, part[:, b * LANES : (b + 1) * LANES], 0.0)
            one = one.reshape(per, poles, LANES).sum(axis=0)
            bs_ref[b * poles : (b + 1) * poles, at] = one
            slab = one if slab is None else slab * decay + one
        slab_ref[:, at] = slab


def conv_kernel(
    members, poles, blocks, d_ref, q_ref, col_ref, row_ref, bs_ref, inc_ref, skip_ref, g_ref
):
    per = LANES // members
    wide = per * poles
    for sub in range(d_ref.shape[1] // LANES):
        at = slice(sub * LANES, (sub + 1) * LANES)
        rate = col_ref[sub * wide : (sub + 1) * wide, 0:1]
        residue = col_ref[sub * wide : (sub + 1) * wide, 1:2]
        lag = ((BLOCK - iota((wide, BLOCK), 1)) % BLOCK).astype(F32)
        base = (residue * jnp.exp(-rate * lag)).reshape(per, poles, BLOCK).sum(axis=1)
        base = base.astype(BF16).astype(F32)
        causal = iota((BLOCK, BLOCK), 1) <= iota((BLOCK, BLOCK), 0)
        left = []
        for g in range(per):
            rows = jnp.broadcast_to(base[g : g + 1], (BLOCK, BLOCK))
            rows = pltpu.roll(rows, 0, 1, stride=1, stride_axis=0)
            left.append(jnp.where(causal, rows, 0.0).astype(BF16))
        ahead = (iota((BLOCK, wide), 0) + 1).astype(F32)
        at_row = slice(sub * wide, (sub + 1) * wide)
        reach = row_ref[1:2, at_row] * jnp.exp(-row_ref[0:1, at_row] * ahead)
        high, low = split(reach)
        left = jnp.concatenate(left + [high, low, high], axis=1)
        same = iota((wide, LANES), 0) // poles == iota((wide, LANES), 1) // members
        decay = jnp.exp(-lane_rate(rate, same, per, poles) * BLOCK)
        owner = iota((1, LANES), 1) // members
        state = inc_ref[:, at]
        right = []
        for b in range(blocks):
            tile = d_ref[b * BLOCK : (b + 1) * BLOCK, at]
            spread = jnp.where(same, jnp.concatenate([state] * per, axis=0), 0.0)
            s_high, s_low = split(spread)
            masked = [tile * jnp.where(owner == g, 1.0, 0.0).astype(BF16) for g in range(per)]
            right.append(jnp.concatenate(masked + [s_high, s_high, s_low], axis=0))
            if b + 1 < blocks:
                state = state * decay + bs_ref[b * poles : (b + 1) * poles, at]
        conv = jnp.dot(left, jnp.concatenate(right, axis=1), preferred_element_type=F32)
        for b in range(blocks):
            rows = slice(b * BLOCK, (b + 1) * BLOCK)
            whole = conv[:, b * LANES : (b + 1) * LANES] + skip_ref[:, at] * d_ref[rows, at].astype(F32)
            g_ref[sub, rows, :] = (q_ref[rows, at].astype(F32) * whole).astype(BF16)


def states(key, value, col, members, poles):
    rows, width = key.shape
    blocks = rows // BLOCK
    step = STEP
    seq = pl.BlockSpec((rows, step), lambda i: (0, i))
    wide = step // members * poles
    return pl.pallas_call(
        lambda *refs: state_kernel(members, poles, blocks, *refs),
        grid=(width // step,),
        in_specs=[
            seq,
            seq,
            pl.BlockSpec((wide, 2), lambda i: (i, 0)),
        ],
        out_specs=[
            seq,
            pl.BlockSpec((blocks * poles, step), lambda i: (0, i)),
            pl.BlockSpec((poles, step), lambda i: (0, i)),
        ],
        out_shape=[
            jax.ShapeDtypeStruct((rows, width), BF16),
            jax.ShapeDtypeStruct((blocks * poles, width), F32),
            jax.ShapeDtypeStruct((poles, width), F32),
        ],
        compiler_params=params(32),
        cost_estimate=cost(4 * poles * members * rows * width * SCALE, 6 * rows * width),
        name="states",
    )(in_hbm(key), in_hbm(value), col)


def convolve(driven, query, col, row, block_state, incoming, skip, members, poles):
    rows, width = driven.shape
    blocks = rows // BLOCK
    step = STEP
    seq = pl.BlockSpec((rows, step), lambda i: (0, i))
    wide = step // members * poles
    return pl.pallas_call(
        lambda *refs: conv_kernel(members, poles, blocks, *refs),
        grid=(width // step,),
        in_specs=[
            seq,
            seq,
            pl.BlockSpec((wide, 2), lambda i: (i, 0)),
            pl.BlockSpec((2, wide), lambda i: (0, i)),
            pl.BlockSpec((blocks * poles, step), lambda i: (0, i)),
            pl.BlockSpec((poles, step), lambda i: (0, i)),
            pl.BlockSpec((1, step), lambda i: (0, i)),
        ],
        out_specs=pl.BlockSpec((step // LANES, rows, LANES), lambda i: (i, 0, 0)),
        out_shape=jax.ShapeDtypeStruct((width // LANES, rows, LANES), BF16),
        compiler_params=params(32),
        cost_estimate=cost(2 * (BLOCK * LANES // members + 3 * LANES) * rows * width * SCALE, 6 * rows * width),
        name="convolve",
    )(in_hbm(driven), in_hbm(query), col, row, block_state, incoming, skip)


def scan_send(total, slabs, width):
    return lax.ppermute(total, "ctx", [(i, i ^ width) for i in range(slabs)])


def pair_total(slab, other, lane, rows, core):
    decay = jnp.exp(-lane * float(rows))
    total = jnp.where(core == 0, slab * decay + other, other * decay + slab)
    half = slab.shape[1] // 2
    return [lax.dynamic_slice_in_dim(a, core * half, half, 1) for a in (total, lane)]


def pairs_ahead(total, lane, rows, slabs):
    pair = lax.axis_index("ctx") // 2
    before = jnp.zeros_like(total)
    for step in range(1, slabs // 2):
        other = scan_send(total, slabs, 2 * step)
        gap = pair - 1 - (pair ^ step)
        decay = jnp.exp(-lane * (jnp.maximum(gap, 0).astype(F32) * float(2 * rows)))
        before = before + jnp.where(gap >= 0, other * decay, 0.0)
    return before


def incoming_state(before, other_half, other_slab, lane, rows, core):
    ahead = jnp.where(
        core == 0,
        jnp.concatenate([before, other_half], axis=1),
        jnp.concatenate([other_half, before], axis=1),
    )
    return jnp.where(core == 0, ahead, ahead * jnp.exp(-lane * float(rows)) + other_slab)


def project_kernel(sizes, sides, started, idx_ref, *refs):
    shards = sum(sizes) // LANES
    gated = [refs[i * shards : (i + 1) * shards] for i in range(sides)]
    refs = refs[sides * shards :]
    weights, refs = refs[: len(sizes)], refs[len(sizes) :]
    totals = [r[...] for r in refs[:sides]] if started else [None] * sides
    outs = refs[-sides:]
    weights, at = list(weights), 0
    while weights:
        depth, rhs = 0, []
        while weights and depth + weights[0].shape[0] <= 2 * LANES:
            rhs.append(weights.pop(0)[...])
            depth += rhs[-1].shape[0]
        rhs = jnp.concatenate(rhs, axis=0) if len(rhs) > 1 else rhs[0]
        for i in range(sides):
            lhs = [r[0] for r in gated[i][at : at + depth // LANES]]
            lhs = jnp.concatenate(lhs, axis=1) if len(lhs) > 1 else lhs[0]
            part = jnp.dot(lhs, rhs, preferred_element_type=F32)
            totals[i] = part if totals[i] is None else totals[i] + part
        at += depth // LANES
    for o_ref, total in zip(outs, totals):
        o_ref[...] = total.astype(o_ref.dtype)


def project(place, ring, gated, pieces, wide, total=None, side=None, dout=None, dtype=F32, cols=COLS):
    shards, rows, depth = gated[0].shape
    steps = [one for _, _, owners in pieces for one in owners]
    sizes = [LANES * len(owners) for _, _, owners in pieces]
    sides = len(gated)
    nb = wide // cols
    idx = shard_table(place, ring, steps)
    if side is not None:
        idx = jnp.concatenate([idx, (side * nb).astype(jnp.int32)[None]])
    block = pl.BlockSpec((rows, cols), lambda b, i: (0, b))
    specs = [pl.BlockSpec((1, rows, depth), lambda b, i, p=p: (i[p], 0, 0)) for p in range(len(steps))] * sides
    specs += [
        pl.BlockSpec((size, cols), lambda b, i, at=at: (at, b)) for size, (_, at, _) in zip(sizes, pieces)
    ]
    operands = [g for g in gated for _ in steps] + [a for a, _, _ in pieces]
    if total is not None:
        specs += [block] * sides
        operands += list(total)
    operands = [in_hbm(a) for a in operands]
    last = len(steps)
    shape = jax.ShapeDtypeStruct((rows, wide if side is None else dout), dtype)
    return pl.pallas_call(
        lambda *refs: project_kernel(sizes, sides, total is not None, *refs),
        grid_spec=pltpu.PrefetchScalarGridSpec(
            num_scalar_prefetch=1,
            grid=(nb,),
            in_specs=specs,
            out_specs=[block if side is None else pl.BlockSpec((rows, cols), lambda b, i: (0, i[last] + b))] * sides,
        ),
        out_shape=[shape] * sides,
        compiler_params=params(48),
        cost_estimate=cost(2 * len(steps) * LANES * sides * rows * wide * SCALE, 4 * sides * rows * wide),
        name="project",
    )(idx, *operands)


def local(mesh_shape, query_stream, key_stream, value_stream, pole_rate, residue, skip_gain, out_weight):
    seqs, rows, width = query_stream.shape
    groups, poles = pole_rate.shape
    members = width // groups
    slabs = mesh_shape["ctx"]
    devices = mesh_shape["dp"] * slabs
    depth, dout = out_weight.shape
    query, key, value = [a.reshape(rows, width) for a in (query_stream, key_stream, value_stream)]
    skip = skip_gain[None]

    if depth != LANES or devices != 32:
        core = lax.axis_index("ctx") % 2
        col, lane = columns(pole_rate, residue), lanes(pole_rate, members)
        driven, block_state, slab = states(key, value, col, members, poles)
        other_slab = scan_send(slab, slabs, 1)
        total, lane_half = pair_total(slab, other_slab, lane, rows, core)
        before = pairs_ahead(total, lane_half, rows, slabs)
        incoming = incoming_state(before, scan_send(before, slabs, 1), other_slab, lane, rows, core)
        gated = convolve(driven, query, col, col.T, block_state, incoming, skip, members, poles)
        weight = lax.all_gather(out_weight, AXES, axis=0, tiled=True)
        flat = gated.transpose(1, 0, 2).reshape(rows, width)
        out = jnp.dot(flat, weight, preferred_element_type=F32)
        return out.astype(BF16).reshape(seqs, rows, dout)

    def swap(a, bit):
        return lax.ppermute(a, AXES, [(i, i ^ bit) for i in range(devices)])

    def ahead(a):
        return lax.ppermute(a, AXES, [(i, (i + 8) % devices) for i in range(devices)])

    place = lax.axis_index(AXES)
    core = place % 2
    half = dout // 2
    ring = devices // 8
    mine = lax.dynamic_slice_in_dim(out_weight, core * half, half, 1)
    give = lax.dynamic_slice_in_dim(out_weight, (1 - core) * half, half, 1)

    def settle(new, work):
        arrays, work = fence(([a for a, _, _ in new], work))
        return [(a, 0, o) for a, (_, _, o) in zip(arrays, new)], work

    def along_x(a, back, y, k):
        return swap(a, 2), 0, [(back, y, 1, i) for i in k]

    def along_y(a, back, x, k):
        return swap(a, 4), 0, [(back, 1, x, i) for i in k]

    both = (0, 1)
    got = swap(give, 1)
    new = [along_x(mine, 0, 0, (0,)), along_y(mine, 0, 0, (0,)), (ahead(mine), 0, [(1, 0, 0, 0)])]
    driven, block_state, slab = states(key, value, columns(pole_rate, residue), members, poles)
    work = (got, driven, block_state, slab, pole_rate, residue)
    new, (got, driven, block_state, slab, pole_rate, residue) = settle(new, work)
    pieces = [(mine, 0, [(0, 0, 0, 0)]), (got, 0, [(0, 0, 0, 1)])]
    more = [along_x(got, 0, 0, (1,)), along_y(got, 0, 0, (1,)), (ahead(got), 0, [(1, 0, 0, 1)])]
    other_slab = scan_send(slab, slabs, 1)
    lane = lanes(pole_rate, members)
    total, lane_half = pair_total(slab, other_slab, lane, rows, core)
    work = (total, lane_half, other_slab, [a for a, _, _ in new])
    more, (total, lane_half, other_slab, (x_mine, y_mine, z_mine)) = settle(more, work)
    for one, two in zip(new, more):
        pieces += [one, two]
    (x_got, _, _), (y_got, _, _), (z_got, _, _) = more
    new = [
        along_x(y_got, 0, 1, (1,)),
        along_y(x_mine, 0, 1, (0,)),
        along_x(z_mine, 1, 0, (0,)),
        along_y(z_got, 1, 0, (1,)),
        (ahead(jnp.concatenate([z_mine, z_got], axis=0)), 0, [(2, 0, 0, 0), (2, 0, 0, 1)]),
    ]
    before = pairs_ahead(total, lane_half, rows, slabs)
    other_half = scan_send(before, slabs, 1)
    aside = jnp.concatenate([x_got, y_mine], axis=0)
    new, (before, other_half, other_slab, aside) = settle(new, (before, other_half, other_slab, aside))
    pieces += new
    (x_half, _, _), (y_half, _, _), (cur, _, _) = new[2:]
    new = [
        along_x(y_half, 1, 1, (1,)),
        along_y(x_half, 1, 1, (0,)),
        along_x(cur[:depth], 2, 0, (0,)),
        along_y(cur[depth:], 2, 0, (1,)),
        (ahead(cur), 0, [(3, 0, 0, 0), (3, 0, 0, 1)]),
    ]
    incoming = incoming_state(before, other_half, other_slab, lane, rows, core)
    col = columns(pole_rate, residue)
    gated = convolve(driven, query, col, col.T, block_state, incoming, skip, members, poles)
    new, gated = settle(new, gated)
    pieces += new
    (x_half, _, _), (y_half, _, _), (cur, _, _) = new[2:]
    new = [
        along_x(cur, 3, 0, both),
        along_y(cur, 3, 0, both),
        (ahead(aside), 0, [(1, 0, 1, 1), (1, 1, 0, 0)]),
    ]
    peer = swap(gated, 1)
    (sum_own,) = project(place, ring, [gated], pieces, half)
    new, (gated, peer, sum_own, x_half, y_half) = settle(new, (gated, peer, sum_own, x_half, y_half))
    (x_whole, _, _), (y_whole, _, _), (aside, _, _) = new
    late = [
        along_x(y_half, 2, 1, (1,)),
        along_y(x_half, 2, 1, (0,)),
        along_x(y_whole[depth:], 3, 1, (1,)),
        along_y(x_whole[:depth], 3, 1, (0,)),
        (ahead(aside), 0, [(2, 0, 1, 1), (2, 1, 0, 0)]),
    ]
    (sum_own,) = project(place, ring, [gated], new, half, [sum_own], cols=2 * COLS)
    (sum_peer,) = project(place, ring, [peer], pieces + new, half)
    late, (gated, peer, sum_own, sum_peer) = settle(late, (gated, peer, sum_own, sum_peer))
    (out_peer,) = project(place, ring, [peer], late, half, [sum_peer], dtype=BF16, cols=2 * COLS)
    other = swap(out_peer, 1)
    (out,) = project(place, ring, [gated], late, half, [sum_own], core, dout, dtype=BF16, cols=2 * COLS)
    return put(other, 1 - core, out).reshape(seqs, rows, dout)


def put_kernel(side_ref, half_ref, whole_ref, o_ref):
    o_ref[...] = half_ref[...]


def put(half, side, whole):
    rows, wide = half.shape
    nb = wide // COLS
    return pl.pallas_call(
        put_kernel,
        grid_spec=pltpu.PrefetchScalarGridSpec(
            num_scalar_prefetch=1,
            grid=(nb,),
            in_specs=[pl.BlockSpec((rows, COLS), lambda b, i: (0, b)), pl.BlockSpec(memory_space=pl.ANY)],
            out_specs=pl.BlockSpec((rows, COLS), lambda b, i: (0, i[0] * nb + b)),
        ),
        out_shape=jax.ShapeDtypeStruct(whole.shape, whole.dtype),
        input_output_aliases={2: 0},
        compiler_params=params(32),
        name="put",
    )(side.astype(jnp.int32)[None], half, whole)


def columns(pole_rate, residue):
    return jnp.stack([pole_rate.reshape(-1), residue.reshape(-1)], axis=1)


def lanes(pole_rate, members):
    return jnp.repeat(pole_rate.T, members, axis=1)


def shard_table(place, ring, steps):
    steps = np.asarray(steps, np.int32)
    z = (place // 8 + ring - steps[:, 0]) % ring
    low = (place % 8) ^ jnp.asarray(steps[:, 1] * 4 + steps[:, 2] * 2 + steps[:, 3])
    return (z * 8 + low).astype(jnp.int32)


def solution(mesh):
    shape = dict(mesh.shape)
    return jax.shard_map(
        lambda *args: local(shape, *args),
        mesh=mesh,
        in_specs=(
            P("dp", "ctx", None),
            P("dp", "ctx", None),
            P("dp", "ctx", None),
            P(),
            P(),
            P(),
            P(("dp", "ctx"), None),
        ),
        out_specs=P("dp", "ctx", None),
        check_vma=False,
    )
```

```python
import jax
import jax.numpy as jnp
import numpy as np
from jax import lax
from jax.experimental import pallas as pl
from jax.experimental.pallas import tpu as pltpu
from jax.sharding import PartitionSpec as P

BLOCK = 128
LANES = 128
COLS = 512
SCALE = 4
STEP = 1024
F32 = jnp.float32
BF16 = jnp.bfloat16
AXES = ("dp", "ctx")
fence = lax.optimization_barrier


def params(mib):
    return pltpu.CompilerParams(vmem_limit_bytes=mib << 20, dimension_semantics=("arbitrary",))


def cost(flops, moved):
    return pl.CostEstimate(flops=int(flops), transcendentals=0, bytes_accessed=int(moved))


def split(a):
    high = a.astype(BF16)
    return high, (a - high.astype(F32)).astype(BF16)


def in_hbm(a):
    return pltpu.with_memory_space_constraint(a, pltpu.HBM)


def iota(shape, axis):
    return lax.broadcasted_iota(jnp.int32, shape, axis)


def lane_rate(rate, same, per, poles):
    return jnp.where(same, rate, 0.0).reshape(per, poles, same.shape[1]).sum(axis=0)


def state_kernel(members, poles, blocks, k_ref, v_ref, col_ref, d_ref, bs_ref, slab_ref):
    per = LANES // members
    wide = per * poles
    back = (BLOCK - 1 - iota((wide, BLOCK), 1)).astype(F32)
    same = iota((wide, LANES), 0) // poles == iota((wide, LANES), 1) // members
    for sub in range(k_ref.shape[1] // LANES):
        at = slice(sub * LANES, (sub + 1) * LANES)
        d = (k_ref[:, at].astype(F32) * v_ref[:, at].astype(F32)).astype(BF16)
        d_ref[:, at] = d
        rate = col_ref[sub * wide : (sub + 1) * wide, 0:1]
        ending = jnp.concatenate(split(jnp.exp(-rate * back)), axis=1)
        tiles = jnp.concatenate([d[b * BLOCK : (b + 1) * BLOCK] for b in range(blocks)], axis=1)
        tiles = jnp.concatenate([tiles, tiles], axis=0)
        part = jnp.dot(ending, tiles, preferred_element_type=F32)
        decay = jnp.exp(-lane_rate(rate, same, per, poles) * BLOCK)
        slab = None
        for b in range(blocks):
            one = jnp.where(same, part[:, b * LANES : (b + 1) * LANES], 0.0)
            one = one.reshape(per, poles, LANES).sum(axis=0)
            bs_ref[b * poles : (b + 1) * poles, at] = one
            slab = one if slab is None else slab * decay + one
        slab_ref[:, at] = slab


def conv_kernel(
    members, poles, blocks, d_ref, q_ref, col_ref, row_ref, bs_ref, inc_ref, skip_ref, g_ref
):
    per = LANES // members
    wide = per * poles
    for sub in range(d_ref.shape[1] // LANES):
        at = slice(sub * LANES, (sub + 1) * LANES)
        rate = col_ref[sub * wide : (sub + 1) * wide, 0:1]
        residue = col_ref[sub * wide : (sub + 1) * wide, 1:2]
        lag = ((BLOCK - iota((wide, BLOCK), 1)) % BLOCK).astype(F32)
        base = (residue * jnp.exp(-rate * lag)).reshape(per, poles, BLOCK).sum(axis=1)
        base = base.astype(BF16).astype(F32)
        causal = iota((BLOCK, BLOCK), 1) <= iota((BLOCK, BLOCK), 0)
        left = []
        for g in range(per):
            rows = jnp.broadcast_to(base[g : g + 1], (BLOCK, BLOCK))
            rows = pltpu.roll(rows, 0, 1, stride=1, stride_axis=0)
            left.append(jnp.where(causal, rows, 0.0).astype(BF16))
        ahead = (iota((BLOCK, wide), 0) + 1).astype(F32)
        at_row = slice(sub * wide, (sub + 1) * wide)
        reach = row_ref[1:2, at_row] * jnp.exp(-row_ref[0:1, at_row] * ahead)
        high, low = split(reach)
        left = jnp.concatenate(left + [high, low, high], axis=1)
        same = iota((wide, LANES), 0) // poles == iota((wide, LANES), 1) // members
        decay = jnp.exp(-lane_rate(rate, same, per, poles) * BLOCK)
        owner = iota((1, LANES), 1) // members
        state = inc_ref[:, at]
        right = []
        for b in range(blocks):
            tile = d_ref[b * BLOCK : (b + 1) * BLOCK, at]
            spread = jnp.where(same, jnp.concatenate([state] * per, axis=0), 0.0)
            s_high, s_low = split(spread)
            masked = [tile * jnp.where(owner == g, 1.0, 0.0).astype(BF16) for g in range(per)]
            right.append(jnp.concatenate(masked + [s_high, s_high, s_low], axis=0))
            if b + 1 < blocks:
                state = state * decay + bs_ref[b * poles : (b + 1) * poles, at]
        conv = jnp.dot(left, jnp.concatenate(right, axis=1), preferred_element_type=F32)
        for b in range(blocks):
            rows = slice(b * BLOCK, (b + 1) * BLOCK)
            whole = conv[:, b * LANES : (b + 1) * LANES] + skip_ref[:, at] * d_ref[rows, at].astype(F32)
            g_ref[sub, rows, :] = (q_ref[rows, at].astype(F32) * whole).astype(BF16)


def states(key, value, col, members, poles):
    rows, width = key.shape
    blocks = rows // BLOCK
    step = STEP
    seq = pl.BlockSpec((rows, step), lambda i: (0, i))
    wide = step // members * poles
    return pl.pallas_call(
        lambda *refs: state_kernel(members, poles, blocks, *refs),
        grid=(width // step,),
        in_specs=[
            seq,
            seq,
            pl.BlockSpec((wide, 2), lambda i: (i, 0)),
        ],
        out_specs=[
            seq,
            pl.BlockSpec((blocks * poles, step), lambda i: (0, i)),
            pl.BlockSpec((poles, step), lambda i: (0, i)),
        ],
        out_shape=[
            pltpu.HBM((rows, width), BF16),
            jax.ShapeDtypeStruct((blocks * poles, width), F32),
            jax.ShapeDtypeStruct((poles, width), F32),
        ],
        compiler_params=params(32),
        cost_estimate=cost(4 * poles * members * rows * width * SCALE, 6 * rows * width),
        name="states",
    )(in_hbm(key), in_hbm(value), col)


def convolve(driven, query, col, row, block_state, incoming, skip, members, poles):
    rows, width = driven.shape
    blocks = rows // BLOCK
    step = STEP
    seq = pl.BlockSpec((rows, step), lambda i: (0, i))
    wide = step // members * poles
    return pl.pallas_call(
        lambda *refs: conv_kernel(members, poles, blocks, *refs),
        grid=(width // step,),
        in_specs=[
            seq,
            seq,
            pl.BlockSpec((wide, 2), lambda i: (i, 0)),
            pl.BlockSpec((2, wide), lambda i: (0, i)),
            pl.BlockSpec((blocks * poles, step), lambda i: (0, i)),
            pl.BlockSpec((poles, step), lambda i: (0, i)),
            pl.BlockSpec((1, step), lambda i: (0, i)),
        ],
        out_specs=pl.BlockSpec((step // LANES, rows, LANES), lambda i: (i, 0, 0)),
        out_shape=jax.ShapeDtypeStruct((width // LANES, rows, LANES), BF16),
        compiler_params=params(32),
        cost_estimate=cost(2 * (BLOCK * LANES // members + 3 * LANES) * rows * width * SCALE, 6 * rows * width),
        name="convolve",
    )(in_hbm(driven), in_hbm(query), col, row, block_state, incoming, skip)


def scan_send(total, slabs, width):
    return lax.ppermute(total, "ctx", [(i, i ^ width) for i in range(slabs)])


def pair_total(slab, other, lane, rows, core):
    decay = jnp.exp(-lane * float(rows))
    total = jnp.where(core == 0, slab * decay + other, other * decay + slab)
    half = slab.shape[1] // 2
    return [lax.dynamic_slice_in_dim(a, core * half, half, 1) for a in (total, lane)]


def pairs_ahead(total, lane, rows, slabs):
    pair = lax.axis_index("ctx") // 2
    before = jnp.zeros_like(total)
    for step in range(1, slabs // 2):
        other = scan_send(total, slabs, 2 * step)
        gap = pair - 1 - (pair ^ step)
        decay = jnp.exp(-lane * (jnp.maximum(gap, 0).astype(F32) * float(2 * rows)))
        before = before + jnp.where(gap >= 0, other * decay, 0.0)
    return before


def incoming_state(before, other_half, other_slab, lane, rows, core):
    ahead = jnp.where(
        core == 0,
        jnp.concatenate([before, other_half], axis=1),
        jnp.concatenate([other_half, before], axis=1),
    )
    return jnp.where(core == 0, ahead, ahead * jnp.exp(-lane * float(rows)) + other_slab)


def project_kernel(sizes, sides, started, idx_ref, *refs):
    shards = sum(sizes) // LANES
    gated = [refs[i * shards : (i + 1) * shards] for i in range(sides)]
    refs = refs[sides * shards :]
    weights, refs = refs[: len(sizes)], refs[len(sizes) :]
    totals = [r[...] for r in refs[:sides]] if started else [None] * sides
    outs = refs[-sides:]
    weights, at = list(weights), 0
    while weights:
        depth, rhs = 0, []
        while weights and depth + weights[0].shape[0] <= 2 * LANES:
            rhs.append(weights.pop(0)[...])
            depth += rhs[-1].shape[0]
        rhs = jnp.concatenate(rhs, axis=0) if len(rhs) > 1 else rhs[0]
        for i in range(sides):
            lhs = [r[0] for r in gated[i][at : at + depth // LANES]]
            lhs = jnp.concatenate(lhs, axis=1) if len(lhs) > 1 else lhs[0]
            part = jnp.dot(lhs, rhs, preferred_element_type=F32)
            totals[i] = part if totals[i] is None else totals[i] + part
        at += depth // LANES
    for o_ref, total in zip(outs, totals):
        o_ref[...] = total.astype(o_ref.dtype)


def project(place, ring, gated, pieces, wide, total=None, side=None, dout=None, dtype=F32, cols=COLS, free=0):
    shards, rows, depth = gated[0].shape
    steps = [one for _, _, owners in pieces for one in owners]
    sizes = [LANES * len(owners) for _, _, owners in pieces]
    sides = len(gated)
    nb = wide // cols
    idx = shard_table(place, ring, steps)
    if side is not None:
        idx = jnp.concatenate([idx, (side * nb).astype(jnp.int32)[None]])
    block = pl.BlockSpec((rows, cols), lambda b, i: (0, b))
    specs = [pl.BlockSpec((1, rows, depth), lambda b, i, p=p: (i[p], 0, 0)) for p in range(len(steps))] * sides
    specs += [
        pl.BlockSpec((size, cols), lambda b, i, at=at: (at, b)) for size, (_, at, _) in zip(sizes, pieces)
    ]
    operands = [g for g in gated for _ in steps] + [a for a, _, _ in pieces]
    operands = [in_hbm(a) for a in operands[: len(operands) - free]] + operands[len(operands) - free :]
    if total is not None:
        specs += [block] * sides
        operands += list(total)
    last = len(steps)
    shape = jax.ShapeDtypeStruct((rows, wide), dtype) if side is None else pltpu.HBM((rows, dout), dtype)
    return pl.pallas_call(
        lambda *refs: project_kernel(sizes, sides, total is not None, *refs),
        grid_spec=pltpu.PrefetchScalarGridSpec(
            num_scalar_prefetch=1,
            grid=(nb,),
            in_specs=specs,
            out_specs=[block if side is None else pl.BlockSpec((rows, cols), lambda b, i: (0, i[last] + b))] * sides,
        ),
        out_shape=[shape] * sides,
        compiler_params=params(48),
        cost_estimate=cost(2 * len(steps) * LANES * sides * rows * wide * SCALE, 4 * sides * rows * wide),
        name="project",
    )(idx, *operands)


def local(mesh_shape, query_stream, key_stream, value_stream, pole_rate, residue, skip_gain, out_weight):
    seqs, rows, width = query_stream.shape
    groups, poles = pole_rate.shape
    members = width // groups
    slabs = mesh_shape["ctx"]
    devices = mesh_shape["dp"] * slabs
    depth, dout = out_weight.shape
    query, key, value = [a.reshape(rows, width) for a in (query_stream, key_stream, value_stream)]
    skip = skip_gain[None]

    if depth != LANES or devices != 32:
        core = lax.axis_index("ctx") % 2
        col, lane = columns(pole_rate, residue), lanes(pole_rate, members)
        driven, block_state, slab = states(key, value, col, members, poles)
        other_slab = scan_send(slab, slabs, 1)
        total, lane_half = pair_total(slab, other_slab, lane, rows, core)
        before = pairs_ahead(total, lane_half, rows, slabs)
        incoming = incoming_state(before, scan_send(before, slabs, 1), other_slab, lane, rows, core)
        gated = convolve(driven, query, col, col.T, block_state, incoming, skip, members, poles)
        weight = lax.all_gather(out_weight, AXES, axis=0, tiled=True)
        flat = gated.transpose(1, 0, 2).reshape(rows, width)
        out = jnp.dot(flat, weight, preferred_element_type=F32)
        return out.astype(BF16).reshape(seqs, rows, dout)

    def swap(a, bit):
        return lax.ppermute(a, AXES, [(i, i ^ bit) for i in range(devices)])

    def ahead(a):
        return lax.ppermute(a, AXES, [(i, (i + 8) % devices) for i in range(devices)])

    place = lax.axis_index(AXES)
    core = place % 2
    half = dout // 2
    ring = devices // 8
    mine = lax.dynamic_slice_in_dim(out_weight, core * half, half, 1)
    give = lax.dynamic_slice_in_dim(out_weight, (1 - core) * half, half, 1)

    def settle(new, work):
        arrays, work = fence(([a for a, _, _ in new], work))
        return [(a, 0, o) for a, (_, _, o) in zip(arrays, new)], work

    def along_x(a, back, y, k):
        return swap(a, 2), 0, [(back, y, 1, i) for i in k]

    def along_y(a, back, x, k):
        return swap(a, 4), 0, [(back, 1, x, i) for i in k]

    both = (0, 1)
    got = swap(give, 1)
    new = [along_x(mine, 0, 0, (0,)), along_y(mine, 0, 0, (0,)), (ahead(mine), 0, [(1, 0, 0, 0)])]
    driven, block_state, slab = states(key, value, columns(pole_rate, residue), members, poles)
    work = (got, driven, block_state, slab, pole_rate, residue)
    new, (got, driven, block_state, slab, pole_rate, residue) = settle(new, work)
    pieces = [(mine, 0, [(0, 0, 0, 0)]), (got, 0, [(0, 0, 0, 1)])]
    more = [along_x(got, 0, 0, (1,)), along_y(got, 0, 0, (1,)), (ahead(got), 0, [(1, 0, 0, 1)])]
    other_slab = scan_send(slab, slabs, 1)
    lane = lanes(pole_rate, members)
    total, lane_half = pair_total(slab, other_slab, lane, rows, core)
    work = (total, lane_half, other_slab, [a for a, _, _ in new])
    more, (total, lane_half, other_slab, (x_mine, y_mine, z_mine)) = settle(more, work)
    for one, two in zip(new, more):
        pieces += [one, two]
    (x_got, _, _), (y_got, _, _), (z_got, _, _) = more
    new = [
        along_x(y_got, 0, 1, (1,)),
        along_y(x_mine, 0, 1, (0,)),
        along_x(z_mine, 1, 0, (0,)),
        along_y(z_got, 1, 0, (1,)),
        (ahead(jnp.concatenate([z_mine, z_got], axis=0)), 0, [(2, 0, 0, 0), (2, 0, 0, 1)]),
    ]
    before = pairs_ahead(total, lane_half, rows, slabs)
    other_half = scan_send(before, slabs, 1)
    aside = jnp.concatenate([x_got, y_mine], axis=0)
    new, (before, other_half, other_slab, aside) = settle(new, (before, other_half, other_slab, aside))
    pieces += new
    (x_half, _, _), (y_half, _, _), (cur, _, _) = new[2:]
    new = [
        along_x(y_half, 1, 1, (1,)),
        along_y(x_half, 1, 1, (0,)),
        along_x(cur[:depth], 2, 0, (0,)),
        along_y(cur[depth:], 2, 0, (1,)),
        (ahead(cur), 0, [(3, 0, 0, 0), (3, 0, 0, 1)]),
    ]
    incoming = incoming_state(before, other_half, other_slab, lane, rows, core)
    col = columns(pole_rate, residue)
    gated = convolve(driven, query, col, col.T, block_state, incoming, skip, members, poles)
    new, gated = settle(new, gated)
    pieces += new
    (x_half, _, _), (y_half, _, _), (cur, _, _) = new[2:]
    new = [
        along_x(cur, 3, 0, both),
        along_y(cur, 3, 0, both),
        (ahead(aside), 0, [(1, 0, 1, 1), (1, 1, 0, 0)]),
    ]
    peer = swap(gated, 1)
    (sum_own,) = project(place, ring, [gated], pieces, half, free=5)
    new, (gated, peer, sum_own, x_half, y_half) = settle(new, (gated, peer, sum_own, x_half, y_half))
    (x_whole, _, _), (y_whole, _, _), (aside, _, _) = new
    (sum_own,) = project(place, ring, [gated], new, half, [sum_own], cols=2 * COLS, free=3)
    over_x, over_y, sum_own = fence((y_whole, x_whole, sum_own))
    over_x, over_y = over_x[depth:], over_y[:depth]
    late = [
        along_x(y_half, 2, 1, (1,)),
        along_y(x_half, 2, 1, (0,)),
        along_x(over_x, 3, 1, (1,)),
        along_y(over_y, 3, 1, (0,)),
        (ahead(aside), 0, [(2, 0, 1, 1), (2, 1, 0, 0)]),
    ]
    (sum_peer,) = project(place, ring, [peer], pieces + new, half, free=8)
    late, (gated, peer, sum_own, sum_peer) = settle(late, (gated, peer, sum_own, sum_peer))
    (out_peer,) = project(place, ring, [peer], late, half, [sum_peer], dtype=BF16, cols=2 * COLS, free=5)
    other = swap(out_peer, 1)
    (out,) = project(place, ring, [gated], late, half, [sum_own], core, dout, dtype=BF16, cols=2 * COLS, free=5)
    return put(other, 1 - core, out).reshape(seqs, rows, dout)


def put_kernel(side_ref, half_ref, whole_ref, o_ref, sem):
    wide = half_ref.shape[1]
    at = pl.multiple_of(side_ref[0] * wide, wide)
    copy = pltpu.make_async_copy(half_ref, o_ref.at[:, pl.ds(at, wide)], sem)
    copy.start()
    copy.wait()


def put(half, side, whole):
    return pl.pallas_call(
        put_kernel,
        in_specs=[
            pl.BlockSpec(memory_space=pltpu.SMEM),
            pl.BlockSpec(memory_space=pltpu.VMEM),
            pl.BlockSpec(memory_space=pl.ANY),
        ],
        out_specs=pl.BlockSpec(memory_space=pl.ANY),
        out_shape=pltpu.HBM(whole.shape, whole.dtype),
        scratch_shapes=[pltpu.SemaphoreType.DMA(())],
        input_output_aliases={2: 0},
        compiler_params=pltpu.CompilerParams(vmem_limit_bytes=32 << 20),
        name="put",
    )(side.astype(jnp.int32)[None], half, whole)


def columns(pole_rate, residue):
    return jnp.stack([pole_rate.reshape(-1), residue.reshape(-1)], axis=1)


def lanes(pole_rate, members):
    return jnp.repeat(pole_rate.T, members, axis=1)


def shard_table(place, ring, steps):
    steps = np.asarray(steps, np.int32)
    z = (place // 8 + ring - steps[:, 0]) % ring
    low = (place % 8) ^ jnp.asarray(steps[:, 1] * 4 + steps[:, 2] * 2 + steps[:, 3])
    return (z * 8 + low).astype(jnp.int32)


def solution(mesh):
    shape = dict(mesh.shape)
    return jax.shard_map(
        lambda *args: local(shape, *args),
        mesh=mesh,
        in_specs=(
            P("dp", "ctx", None),
            P("dp", "ctx", None),
            P("dp", "ctx", None),
            P(),
            P(),
            P(),
            P(("dp", "ctx"), None),
        ),
        out_specs=P("dp", "ctx", None),
        check_vma=False,
    )
```

```python
import jax
import jax.numpy as jnp
import numpy as np
from jax import lax
from jax.experimental import pallas as pl
from jax.experimental.pallas import tpu as pltpu
from jax.sharding import PartitionSpec as P

BLOCK = 128
LANES = 128
COLS = 512
SCALE = 4
STEP = 1024
F32 = jnp.float32
BF16 = jnp.bfloat16
AXES = ("dp", "ctx")
fence = lax.optimization_barrier


def params(mib):
    return pltpu.CompilerParams(vmem_limit_bytes=mib << 20, dimension_semantics=("arbitrary",))


def cost(flops, moved):
    return pl.CostEstimate(flops=int(flops), transcendentals=0, bytes_accessed=int(moved))


def split(a):
    high = a.astype(BF16)
    return high, (a - high.astype(F32)).astype(BF16)


def in_hbm(a):
    return pltpu.with_memory_space_constraint(a, pltpu.HBM)


def iota(shape, axis):
    return lax.broadcasted_iota(jnp.int32, shape, axis)


def lane_rate(rate, same, per, poles):
    return jnp.where(same, rate, 0.0).reshape(per, poles, same.shape[1]).sum(axis=0)


def state_kernel(members, poles, blocks, k_ref, v_ref, col_ref, d_ref, bs_ref, slab_ref):
    per = LANES // members
    wide = per * poles
    back = (BLOCK - 1 - iota((wide, BLOCK), 1)).astype(F32)
    same = iota((wide, LANES), 0) // poles == iota((wide, LANES), 1) // members
    for sub in range(k_ref.shape[1] // LANES):
        at = slice(sub * LANES, (sub + 1) * LANES)
        d = (k_ref[:, at].astype(F32) * v_ref[:, at].astype(F32)).astype(BF16)
        d_ref[:, at] = d
        rate = col_ref[sub * wide : (sub + 1) * wide, 0:1]
        ending = jnp.concatenate(split(jnp.exp(-rate * back)), axis=1)
        tiles = jnp.concatenate([d[b * BLOCK : (b + 1) * BLOCK] for b in range(blocks)], axis=1)
        tiles = jnp.concatenate([tiles, tiles], axis=0)
        part = jnp.dot(ending, tiles, preferred_element_type=F32)
        decay = jnp.exp(-lane_rate(rate, same, per, poles) * BLOCK)
        slab = None
        for b in range(blocks):
            one = jnp.where(same, part[:, b * LANES : (b + 1) * LANES], 0.0)
            one = one.reshape(per, poles, LANES).sum(axis=0)
            bs_ref[b * poles : (b + 1) * poles, at] = one
            slab = one if slab is None else slab * decay + one
        slab_ref[:, at] = slab


def conv_kernel(
    members, poles, blocks, d_ref, q_ref, col_ref, row_ref, bs_ref, inc_ref, skip_ref, g_ref
):
    per = LANES // members
    wide = per * poles
    for sub in range(d_ref.shape[1] // LANES):
        at = slice(sub * LANES, (sub + 1) * LANES)
        rate = col_ref[sub * wide : (sub + 1) * wide, 0:1]
        residue = col_ref[sub * wide : (sub + 1) * wide, 1:2]
        lag = ((BLOCK - iota((wide, BLOCK), 1)) % BLOCK).astype(F32)
        base = (residue * jnp.exp(-rate * lag)).reshape(per, poles, BLOCK).sum(axis=1)
        base = base.astype(BF16).astype(F32)
        causal = iota((BLOCK, BLOCK), 1) <= iota((BLOCK, BLOCK), 0)
        left = []
        for g in range(per):
            rows = jnp.broadcast_to(base[g : g + 1], (BLOCK, BLOCK))
            rows = pltpu.roll(rows, 0, 1, stride=1, stride_axis=0)
            left.append(jnp.where(causal, rows, 0.0).astype(BF16))
        ahead = (iota((BLOCK, wide), 0) + 1).astype(F32)
        at_row = slice(sub * wide, (sub + 1) * wide)
        reach = row_ref[1:2, at_row] * jnp.exp(-row_ref[0:1, at_row] * ahead)
        high, low = split(reach)
        left = jnp.concatenate(left + [high, low, high], axis=1)
        same = iota((wide, LANES), 0) // poles == iota((wide, LANES), 1) // members
        decay = jnp.exp(-lane_rate(rate, same, per, poles) * BLOCK)
        owner = iota((1, LANES), 1) // members
        state = inc_ref[:, at]
        right = []
        for b in range(blocks):
            tile = d_ref[b * BLOCK : (b + 1) * BLOCK, at]
            spread = jnp.where(same, jnp.concatenate([state] * per, axis=0), 0.0)
            s_high, s_low = split(spread)
            masked = [tile * jnp.where(owner == g, 1.0, 0.0).astype(BF16) for g in range(per)]
            right.append(jnp.concatenate(masked + [s_high, s_high, s_low], axis=0))
            if b + 1 < blocks:
                state = state * decay + bs_ref[b * poles : (b + 1) * poles, at]
        conv = jnp.dot(left, jnp.concatenate(right, axis=1), preferred_element_type=F32)
        for b in range(blocks):
            rows = slice(b * BLOCK, (b + 1) * BLOCK)
            whole = conv[:, b * LANES : (b + 1) * LANES] + skip_ref[:, at] * d_ref[rows, at].astype(F32)
            g_ref[sub, rows, :] = (q_ref[rows, at].astype(F32) * whole).astype(BF16)


def states(key, value, col, members, poles):
    rows, width = key.shape
    blocks = rows // BLOCK
    step = STEP
    seq = pl.BlockSpec((rows, step), lambda i: (0, i))
    wide = step // members * poles
    return pl.pallas_call(
        lambda *refs: state_kernel(members, poles, blocks, *refs),
        grid=(width // step,),
        in_specs=[
            seq,
            seq,
            pl.BlockSpec((wide, 2), lambda i: (i, 0)),
        ],
        out_specs=[
            seq,
            pl.BlockSpec((blocks * poles, step), lambda i: (0, i)),
            pl.BlockSpec((poles, step), lambda i: (0, i)),
        ],
        out_shape=[
            pltpu.HBM((rows, width), BF16),
            jax.ShapeDtypeStruct((blocks * poles, width), F32),
            jax.ShapeDtypeStruct((poles, width), F32),
        ],
        compiler_params=params(32),
        cost_estimate=cost(4 * poles * members * rows * width * SCALE, 6 * rows * width),
        name="states",
    )(in_hbm(key), in_hbm(value), col)


def convolve(driven, query, col, row, block_state, incoming, skip, members, poles):
    rows, width = driven.shape
    blocks = rows // BLOCK
    step = STEP
    seq = pl.BlockSpec((rows, step), lambda i: (0, i))
    wide = step // members * poles
    return pl.pallas_call(
        lambda *refs: conv_kernel(members, poles, blocks, *refs),
        grid=(width // step,),
        in_specs=[
            seq,
            seq,
            pl.BlockSpec((wide, 2), lambda i: (i, 0)),
            pl.BlockSpec((2, wide), lambda i: (0, i)),
            pl.BlockSpec((blocks * poles, step), lambda i: (0, i)),
            pl.BlockSpec((poles, step), lambda i: (0, i)),
            pl.BlockSpec((1, step), lambda i: (0, i)),
        ],
        out_specs=pl.BlockSpec((step // LANES, rows, LANES), lambda i: (i, 0, 0)),
        out_shape=jax.ShapeDtypeStruct((width // LANES, rows, LANES), BF16),
        compiler_params=params(32),
        cost_estimate=cost(2 * (BLOCK * LANES // members + 3 * LANES) * rows * width * 3 * SCALE, 6 * rows * width),
        name="convolve",
    )(in_hbm(driven), in_hbm(query), col, row, block_state, incoming, skip)


def scan_send(total, slabs, width):
    return lax.ppermute(total, "ctx", [(i, i ^ width) for i in range(slabs)])


def pair_total(slab, other, lane, rows, core):
    decay = jnp.exp(-lane * float(rows))
    total = jnp.where(core == 0, slab * decay + other, other * decay + slab)
    half = slab.shape[1] // 2
    return [lax.dynamic_slice_in_dim(a, core * half, half, 1) for a in (total, lane)]


def pairs_ahead(total, lane, rows, slabs):
    pair = lax.axis_index("ctx") // 2
    before = jnp.zeros_like(total)
    for step in range(1, slabs // 2):
        other = scan_send(total, slabs, 2 * step)
        gap = pair - 1 - (pair ^ step)
        decay = jnp.exp(-lane * (jnp.maximum(gap, 0).astype(F32) * float(2 * rows)))
        before = before + jnp.where(gap >= 0, other * decay, 0.0)
    return before


def incoming_state(before, other_half, other_slab, lane, rows, core):
    ahead = jnp.where(
        core == 0,
        jnp.concatenate([before, other_half], axis=1),
        jnp.concatenate([other_half, before], axis=1),
    )
    return jnp.where(core == 0, ahead, ahead * jnp.exp(-lane * float(rows)) + other_slab)


def project_kernel(sizes, sides, started, idx_ref, *refs):
    shards = sum(sizes) // LANES
    gated = [refs[i * shards : (i + 1) * shards] for i in range(sides)]
    refs = refs[sides * shards :]
    weights, refs = refs[: len(sizes)], refs[len(sizes) :]
    totals = [r[...] for r in refs[:sides]] if started else [None] * sides
    outs = refs[-sides:]
    weights, at = list(weights), 0
    while weights:
        depth, rhs = 0, []
        while weights and depth + weights[0].shape[0] <= 2 * LANES:
            rhs.append(weights.pop(0)[...])
            depth += rhs[-1].shape[0]
        rhs = jnp.concatenate(rhs, axis=0) if len(rhs) > 1 else rhs[0]
        for i in range(sides):
            lhs = [r[0] for r in gated[i][at : at + depth // LANES]]
            lhs = jnp.concatenate(lhs, axis=1) if len(lhs) > 1 else lhs[0]
            part = jnp.dot(lhs, rhs, preferred_element_type=F32)
            totals[i] = part if totals[i] is None else totals[i] + part
        at += depth // LANES
    for o_ref, total in zip(outs, totals):
        o_ref[...] = total.astype(o_ref.dtype)


def project(place, ring, gated, pieces, wide, total=None, side=None, dout=None, dtype=F32, cols=COLS, free=0):
    shards, rows, depth = gated[0].shape
    steps = [one for _, _, owners in pieces for one in owners]
    sizes = [LANES * len(owners) for _, _, owners in pieces]
    sides = len(gated)
    nb = wide // cols
    idx = shard_table(place, ring, steps)
    if side is not None:
        idx = jnp.concatenate([idx, (side * nb).astype(jnp.int32)[None]])
    block = pl.BlockSpec((rows, cols), lambda b, i: (0, b))
    specs = [pl.BlockSpec((1, rows, depth), lambda b, i, p=p: (i[p], 0, 0)) for p in range(len(steps))] * sides
    specs += [
        pl.BlockSpec((size, cols), lambda b, i, at=at: (at, b)) for size, (_, at, _) in zip(sizes, pieces)
    ]
    operands = [g for g in gated for _ in steps] + [a for a, _, _ in pieces]
    operands = [in_hbm(a) for a in operands[: len(operands) - free]] + operands[len(operands) - free :]
    if total is not None:
        specs += [block] * sides
        operands += list(total)
    last = len(steps)
    shape = jax.ShapeDtypeStruct((rows, wide), dtype) if side is None else pltpu.HBM((rows, dout), dtype)
    return pl.pallas_call(
        lambda *refs: project_kernel(sizes, sides, total is not None, *refs),
        grid_spec=pltpu.PrefetchScalarGridSpec(
            num_scalar_prefetch=1,
            grid=(nb,),
            in_specs=specs,
            out_specs=[block if side is None else pl.BlockSpec((rows, cols), lambda b, i: (0, i[last] + b))] * sides,
        ),
        out_shape=[shape] * sides,
        compiler_params=params(48),
        cost_estimate=cost(2 * len(steps) * LANES * sides * rows * wide, 4 * sides * rows * wide),
        name="project",
    )(idx, *operands)


def local(mesh_shape, query_stream, key_stream, value_stream, pole_rate, residue, skip_gain, out_weight):
    seqs, rows, width = query_stream.shape
    groups, poles = pole_rate.shape
    members = width // groups
    slabs = mesh_shape["ctx"]
    devices = mesh_shape["dp"] * slabs
    depth, dout = out_weight.shape
    query, key, value = [a.reshape(rows, width) for a in (query_stream, key_stream, value_stream)]
    skip = skip_gain[None]

    if depth != LANES or devices != 32:
        core = lax.axis_index("ctx") % 2
        col, lane = columns(pole_rate, residue), lanes(pole_rate, members)
        driven, block_state, slab = states(key, value, col, members, poles)
        other_slab = scan_send(slab, slabs, 1)
        total, lane_half = pair_total(slab, other_slab, lane, rows, core)
        before = pairs_ahead(total, lane_half, rows, slabs)
        incoming = incoming_state(before, scan_send(before, slabs, 1), other_slab, lane, rows, core)
        gated = convolve(driven, query, col, col.T, block_state, incoming, skip, members, poles)
        weight = lax.all_gather(out_weight, AXES, axis=0, tiled=True)
        flat = gated.transpose(1, 0, 2).reshape(rows, width)
        out = jnp.dot(flat, weight, preferred_element_type=F32)
        return out.astype(BF16).reshape(seqs, rows, dout)

    def swap(a, bit):
        return lax.ppermute(a, AXES, [(i, i ^ bit) for i in range(devices)])

    def ahead(a):
        return lax.ppermute(a, AXES, [(i, (i + 8) % devices) for i in range(devices)])

    place = lax.axis_index(AXES)
    core = place % 2
    half = dout // 2
    ring = devices // 8
    mine = lax.dynamic_slice_in_dim(out_weight, core * half, half, 1)
    give = lax.dynamic_slice_in_dim(out_weight, (1 - core) * half, half, 1)

    def settle(new, work):
        arrays, work = fence(([a for a, _, _ in new], work))
        return [(a, 0, o) for a, (_, _, o) in zip(arrays, new)], work

    def along_x(a, back, y, k):
        return swap(a, 2), 0, [(back, y, 1, i) for i in k]

    def along_y(a, back, x, k):
        return swap(a, 4), 0, [(back, 1, x, i) for i in k]

    both = (0, 1)
    got = swap(give, 1)
    new = [along_x(mine, 0, 0, (0,)), along_y(mine, 0, 0, (0,)), (ahead(mine), 0, [(1, 0, 0, 0)])]
    driven, block_state, slab = states(key, value, columns(pole_rate, residue), members, poles)
    work = (got, driven, block_state, slab, pole_rate, residue)
    new, (got, driven, block_state, slab, pole_rate, residue) = settle(new, work)
    pieces = [(mine, 0, [(0, 0, 0, 0)]), (got, 0, [(0, 0, 0, 1)])]
    more = [along_x(got, 0, 0, (1,)), along_y(got, 0, 0, (1,)), (ahead(got), 0, [(1, 0, 0, 1)])]
    other_slab = scan_send(slab, slabs, 1)
    lane = lanes(pole_rate, members)
    total, lane_half = pair_total(slab, other_slab, lane, rows, core)
    work = (total, lane_half, other_slab, [a for a, _, _ in new])
    more, (total, lane_half, other_slab, (x_mine, y_mine, z_mine)) = settle(more, work)
    for one, two in zip(new, more):
        pieces += [one, two]
    (x_got, _, _), (y_got, _, _), (z_got, _, _) = more
    new = [
        along_x(y_got, 0, 1, (1,)),
        along_y(x_mine, 0, 1, (0,)),
        along_x(z_mine, 1, 0, (0,)),
        along_y(z_got, 1, 0, (1,)),
        (ahead(jnp.concatenate([z_mine, z_got], axis=0)), 0, [(2, 0, 0, 0), (2, 0, 0, 1)]),
    ]
    before = pairs_ahead(total, lane_half, rows, slabs)
    other_half = scan_send(before, slabs, 1)
    aside = jnp.concatenate([x_got, y_mine], axis=0)
    new, (before, other_half, other_slab, aside) = settle(new, (before, other_half, other_slab, aside))
    pieces += new
    (x_half, _, _), (y_half, _, _), (cur, _, _) = new[2:]
    new = [
        along_x(y_half, 1, 1, (1,)),
        along_y(x_half, 1, 1, (0,)),
        along_x(cur[:depth], 2, 0, (0,)),
        along_y(cur[depth:], 2, 0, (1,)),
        (ahead(cur), 0, [(3, 0, 0, 0), (3, 0, 0, 1)]),
    ]
    incoming = incoming_state(before, other_half, other_slab, lane, rows, core)
    col = columns(pole_rate, residue)
    gated = convolve(driven, query, col, col.T, block_state, incoming, skip, members, poles)
    new, gated = settle(new, gated)
    pieces += new
    (x_half, _, _), (y_half, _, _), (cur, _, _) = new[2:]
    new = [
        along_x(cur, 3, 0, both),
        along_y(cur, 3, 0, both),
        (ahead(aside), 0, [(1, 0, 1, 1), (1, 1, 0, 0)]),
    ]
    peer = swap(gated, 1)
    (sum_own,) = project(place, ring, [gated], pieces, half, free=5)
    new, (gated, peer, sum_own, x_half, y_half) = settle(new, (gated, peer, sum_own, x_half, y_half))
    (x_whole, _, _), (y_whole, _, _), (aside, _, _) = new
    (sum_own,) = project(place, ring, [gated], new, half, [sum_own], cols=2 * COLS, free=3)
    over_x, over_y, sum_own = fence((y_whole, x_whole, sum_own))
    over_x, over_y = over_x[depth:], over_y[:depth]
    late = [
        along_x(y_half, 2, 1, (1,)),
        along_y(x_half, 2, 1, (0,)),
        along_x(over_x, 3, 1, (1,)),
        along_y(over_y, 3, 1, (0,)),
        (ahead(aside), 0, [(2, 0, 1, 1), (2, 1, 0, 0)]),
    ]
    (sum_peer,) = project(place, ring, [peer], pieces + new, half, free=8)
    late, (gated, peer, sum_own, sum_peer) = settle(late, (gated, peer, sum_own, sum_peer))
    (out_peer,) = project(place, ring, [peer], late, half, [sum_peer], dtype=BF16, cols=2 * COLS, free=5)
    other = swap(out_peer, 1)
    (out,) = project(place, ring, [gated], late, half, [sum_own], core, dout, dtype=BF16, cols=2 * COLS, free=5)
    return put(other, 1 - core, out).reshape(seqs, rows, dout)


def put_kernel(side_ref, half_ref, whole_ref, o_ref, sem):
    wide = half_ref.shape[1]
    at = pl.multiple_of(side_ref[0] * wide, wide)
    copy = pltpu.make_async_copy(half_ref, o_ref.at[:, pl.ds(at, wide)], sem)
    copy.start()
    copy.wait()


def put(half, side, whole):
    return pl.pallas_call(
        put_kernel,
        in_specs=[
            pl.BlockSpec(memory_space=pltpu.SMEM),
            pl.BlockSpec(memory_space=pltpu.VMEM),
            pl.BlockSpec(memory_space=pl.ANY),
        ],
        out_specs=pl.BlockSpec(memory_space=pl.ANY),
        out_shape=pltpu.HBM(whole.shape, whole.dtype),
        scratch_shapes=[pltpu.SemaphoreType.DMA(())],
        input_output_aliases={2: 0},
        compiler_params=pltpu.CompilerParams(vmem_limit_bytes=32 << 20),
        name="put",
    )(side.astype(jnp.int32)[None], half, whole)


def columns(pole_rate, residue):
    return jnp.stack([pole_rate.reshape(-1), residue.reshape(-1)], axis=1)


def lanes(pole_rate, members):
    return jnp.repeat(pole_rate.T, members, axis=1)


def shard_table(place, ring, steps):
    steps = np.asarray(steps, np.int32)
    z = (place // 8 + ring - steps[:, 0]) % ring
    low = (place % 8) ^ jnp.asarray(steps[:, 1] * 4 + steps[:, 2] * 2 + steps[:, 3])
    return (z * 8 + low).astype(jnp.int32)


def solution(mesh):
    shape = dict(mesh.shape)
    return jax.shard_map(
        lambda *args: local(shape, *args),
        mesh=mesh,
        in_specs=(
            P("dp", "ctx", None),
            P("dp", "ctx", None),
            P("dp", "ctx", None),
            P(),
            P(),
            P(),
            P(("dp", "ctx"), None),
        ),
        out_specs=P("dp", "ctx", None),
        check_vma=False,
    )
```
